32 devices in a mesh: orb: 8 (over z, y), slab: 4 (over x, core).
Axes of the slice: x: 2, y: 2, z: 4, core: 2. Of those that a mesh axis runs over, the one named last changes fastest.
Arguments:
- orbitals: float32 [2, 1024, 16384], P(None, 'orb', 'slab'), may hold values from -1.5 to 1.5
- offsets: int32 [1024], replicated, may hold values from 0 to 1472, as said below
- pairs: int32 [8, 3], P('orb'), may hold values from 0 to 1, as said below
- kernel: float32 [8, 3, 128, 128], P('orb'), may hold values from -0.6 to 0.6
Outputs:
- gradient: float32 [1024, 16384], P('orb', 'slab')
The draws below stay inside these ranges and needn't reach their ends.
Inputs may be any that keep to these rules, and one draw needn't show every extreme that they name: offsets[f] lies between 192 * (f // 128) and 192 * (f // 128) + 128; in every block the first function's offset is the low end and the second function's the high end. pairs[A, 1] is 1; the list is symmetric, pairs[A, 1 + k] = pairs[A + k, 1 - k]; entries whose block A + k lies outside 0 to 7 are 0.
All inputs are finite; a program needn't handle non-finite values.
Results may differ from the reference program's by a relative error of at most 0.0003.
Values sent between devices are 32-bit elements; how exact they have to be, the bound alone decides.
No kernel may reach another device: no remote copies, remote signals or barrier semaphores. Data moves between devices by JAX's collectives and lax.ppermute only.
A program may use at most 128 MiB of HBM per device.

```python
import math
import jax
import jax.numpy as jnp
from jax import lax

BLOCK_FUNCTIONS = 128
PATCH = 256
SPREAD = 128
SLOT_COUNT = 3
BSTEP = 192
SEG = 16384
NF = 1024
BLOCK_TOTAL = 8


def draw_offsets(key, part):
    rows_all = jnp.arange(NF, dtype=jnp.int32)
    within = rows_all % BLOCK_FUNCTIONS
    spread_draw = jax.random.randint(key, (NF,), 0, SPREAD + 1, dtype=jnp.int32)
    spread_draw = jnp.where(within == 0, 0, jnp.where(within == 1, SPREAD, spread_draw))
    return (BSTEP * (rows_all // BLOCK_FUNCTIONS) + spread_draw).astype(jnp.int32)


def draw_pairs(key, part):
    blocks_within_reach = (SLOT_COUNT - 1) // 2
    listed = (jax.random.randint(key, (BLOCK_TOTAL, blocks_within_reach), 0, 4, dtype=jnp.int32) > 0).astype(jnp.int32)
    blocks_all = jnp.arange(BLOCK_TOTAL, dtype=jnp.int32)
    columns = []
    for block_distance in range(-blocks_within_reach, blocks_within_reach + 1):
        if block_distance == 0:
            columns.append(jnp.ones((BLOCK_TOTAL,), jnp.int32))
        elif block_distance > 0:
            inside = blocks_all + block_distance < BLOCK_TOTAL
            columns.append(jnp.where(inside, listed[:, block_distance - 1], 0).astype(jnp.int32))
        else:
            inside = blocks_all + block_distance >= 0
            columns.append(jnp.where(inside, jnp.roll(listed[:, -block_distance - 1], -block_distance), 0).astype(jnp.int32))
    return jnp.stack(columns, axis=1)


def level_of(own_key, extent, cuts, low, top_value):
    loudness, own = 1.0, jax.random.fold_in(own_key, 6)
    for axis_at, parts in cuts:
        heights = jnp.exp(jax.random.uniform(jax.random.fold_in(own, axis_at), (parts,), jnp.float32, low / len(cuts), top_value / len(cuts)))
        loudness = loudness * jnp.repeat(heights, extent[axis_at] // parts).reshape([-1 if axis == axis_at else 1 for axis in range(len(extent))])
    return loudness


def centred(rng, dims, deviation, limit, shards=(), kind=jnp.bfloat16):
    values = jax.random.normal(rng, dims, jnp.float32) * deviation
    if len(shards) > 0:
        values = level_of(rng, dims, shards, -0.22, 0.18) * values
    return jnp.clip(values, min=-limit, max=limit).astype(kind)


def setup_inputs(seed: int = 0) -> dict:
    streams_of = jax.random.split(jax.random.key(seed), 5)
    orbitals = centred(streams_of[0], (2, NF, SEG), 0.25, 1.5, ((1, 8), (2, 4)), jnp.float32)
    offsets = draw_offsets(jax.random.fold_in(streams_of[4], 71), 0)
    pairs = draw_pairs(jax.random.fold_in(streams_of[4], 71), 0)
    kernel = centred(streams_of[3], (BLOCK_TOTAL, SLOT_COUNT, BLOCK_FUNCTIONS, BLOCK_FUNCTIONS), 0.1, 0.6, ((0, 8),), jnp.float32)
    return {"orbitals": orbitals, "offsets": offsets, "pairs": pairs, "kernel": kernel}


def position_row(segment, column_shift, window):
    blank = jnp.zeros((segment.shape[0], window), segment.dtype)
    return lax.dynamic_update_slice(blank, segment, (jnp.int32(0), column_shift))

def place_rows(segments, shifts, window):

    def inner(member_rows):
        return jax.vmap(lambda segment, column_shift: position_row(segment, column_shift, window))(member_rows, shifts)
    return jax.vmap(inner)(segments)

def pick_row(window_row, column_shift, patch):
    return lax.dynamic_slice(window_row, (jnp.int32(0), column_shift), (window_row.shape[0], patch))

def aligned(own_part, near_part, lag_cols):
    window = own_part.shape[-1]
    if lag_cols >= 0:
        return (own_part[..., lag_cols:], near_part[..., :window - lag_cols])
    return (own_part[..., :window + lag_cols], near_part[..., -lag_cols:])

def reference(orbitals, offsets, pairs, kernel):
    members, total_rows, seg_len = orbitals.shape
    planes = seg_len // PATCH
    window = PATCH + SPREAD
    block_count = total_rows // BLOCK_FUNCTIONS
    blocks_within_reach = (pairs.shape[1] - 1) // 2
    rows_all = jnp.arange(total_rows, dtype=jnp.int32)
    shifts = jnp.clip(offsets - BSTEP * (rows_all // BLOCK_FUNCTIONS), 0, SPREAD)
    volume = 1.0 / math.sqrt(SEG)

    def windows_of(block):
        start = (jnp.clip(block, 0, block_count - 1) * BLOCK_FUNCTIONS).astype(jnp.int32)
        block_rows = lax.dynamic_slice_in_dim(orbitals, start, BLOCK_FUNCTIONS, axis=1).reshape(members, BLOCK_FUNCTIONS, planes, PATCH)
        block_shift = lax.dynamic_slice_in_dim(shifts, start, BLOCK_FUNCTIONS)
        return (place_rows(block_rows, block_shift, window), block_shift)

    def one_block(block):
        own_windows, own_shift = windows_of(block)
        pair_row = lax.dynamic_index_in_dim(pairs, block, 0, keepdims=False).astype(jnp.float32)
        kernel_row = lax.dynamic_index_in_dim(kernel, block, 0, keepdims=False)
        accumulated = jnp.zeros((BLOCK_FUNCTIONS, planes, window), jnp.float32)
        for block_distance in range(-blocks_within_reach, blocks_within_reach + 1):
            slot_index = block_distance + blocks_within_reach
            nearby, unused_shift = windows_of(block + block_distance)
            lag_cols = block_distance * BSTEP
            own_part, near_part = aligned(own_windows[0], nearby[1], lag_cols)
            hamilton = volume * jnp.einsum('ixc,jxc->ij', own_part, near_part, precision=lax.Precision.HIGHEST)
            hamilton = hamilton * pair_row[slot_index]
            kernel_block = kernel_row[slot_index] * pair_row[slot_index]
            if lag_cols >= 0:
                target = slice(lag_cols, window)
                source = slice(0, window - lag_cols)
            else:
                target = slice(0, window + lag_cols)
                source = slice(-lag_cols, window)
            contribution = jnp.einsum('ij,jxc->ixc', kernel_block, nearby[1][..., source], precision=lax.Precision.HIGHEST)
            contribution = contribution - jnp.einsum('ij,jxc->ixc', hamilton, nearby[0][..., source], precision=lax.Precision.HIGHEST)
            accumulated = accumulated.at[..., target].add(contribution)
        picked = jax.vmap(lambda window_row, column_shift: pick_row(window_row, column_shift, PATCH))(accumulated, own_shift)
        return picked.reshape(BLOCK_FUNCTIONS, planes * PATCH)
    result = lax.map(one_block, jnp.arange(block_count, dtype=jnp.int32))
    return result.reshape(total_rows, seg_len)
```

```python
import functools
import math

import jax
import jax.numpy as jnp
from jax import lax
from jax.experimental import pallas as pl
from jax.experimental.pallas import tpu as pltpu
from jax.sharding import PartitionSpec as P

BLOCK_FUNCTIONS = 128
PATCH = 256
SPREAD = 128
REACH = 1
BSTEP = 192
SEG = 16384
LANES = 128
ROWS = 32
COLUMN_TILES = (PATCH + SPREAD) // LANES
SOURCES = 3


def chunk_bounds(planes, shares):
    bounds, start = [], 0
    for share in shares:
        stop = start + share * planes // 16
        bounds.append((start, stop))
        start = stop
    return bounds


def lane_turn(values, index):
    return jnp.take_along_axis(values, index, axis=1)


def split_store(hi_ref, lo_ref, rows, lanes, values):
    high = values.astype(jnp.bfloat16)
    hi_ref[rows, lanes] = high
    lo_ref[rows, lanes] = (values - high.astype(jnp.float32)).astype(jnp.bfloat16)


def placed_tiles(first, second, index, tile_of, own):
    left, right = lane_turn(first, index), lane_turn(second, index)
    zero = jnp.zeros_like(left)
    tiles = []
    for k in range(COLUMN_TILES):
        if own:
            inside = tile_of == 0
            tiles.append(
                (
                    jnp.where(inside, left, zero),
                    jnp.where(inside, right, left),
                    jnp.where(inside, zero, right),
                )[k]
            )
        else:
            tiles.append(jnp.where(tile_of == -k, left, jnp.where(tile_of == 1 - k, right, zero)))
    return tiles


def turn_tables(place_ref, source, rows):
    lane = lax.broadcasted_iota(jnp.int32, (ROWS, LANES), 1)
    ahead = lane - jnp.broadcast_to(place_ref[rows, source : source + 1], (ROWS, LANES))
    return ahead & (LANES - 1), ahead >> 7


def row_groups():
    return [slice(start, start + ROWS) for start in range(0, BLOCK_FUNCTIONS, ROWS)]


NT = (((1,), (1,)), ((), ()))


def gram_kernel(step_planes, place_ref, own_ref, y_ref, z_ref, before_ref, out_ref, l_hi, l_lo, r_hi, r_lo):
    for rows in row_groups():
        for source in range(SOURCES):
            index, tile_of = turn_tables(place_ref, source, rows)
            near = slice(source * BLOCK_FUNCTIONS + rows.start, source * BLOCK_FUNCTIONS + rows.stop)
            for plane in range(step_planes):
                cut = slice(plane * PATCH, plane * PATCH + LANES)
                cut2 = slice(plane * PATCH + LANES, (plane + 1) * PATCH)
                if source == 0:
                    first, second = own_ref[1, rows, cut], own_ref[1, rows, cut2]
                    tiles = placed_tiles(own_ref[0, rows, cut], own_ref[0, rows, cut2], index, tile_of, True)
                    for k in range(COLUMN_TILES):
                        at = (plane * COLUMN_TILES + k) * LANES
                        split_store(l_hi, l_lo, rows, slice(at, at + LANES), tiles[k])
                else:
                    ref = (y_ref, z_ref)[source - 1]
                    first, second = ref[rows, cut], ref[rows, cut2]
                tiles = placed_tiles(first, second, index, tile_of, source == 0)
                for k in range(COLUMN_TILES):
                    at = (plane * COLUMN_TILES + k) * LANES
                    split_store(r_hi, r_lo, near, slice(at, at + LANES), tiles[k])
    dot = functools.partial(lax.dot_general, dimension_numbers=NT, preferred_element_type=jnp.float32)
    total = dot(l_hi[...], r_hi[...]) + (dot(l_hi[...], r_lo[...]) + dot(l_lo[...], r_hi[...]))

    @pl.when(pl.program_id(0) == 0)
    def _():
        out_ref[...] = before_ref[...] + total

    @pl.when(pl.program_id(0) != 0)
    def _():
        out_ref[...] += total


def apply_kernel(
    step_planes, place_ref, mix_ref, near_ref, far_ref, weight_ref, own_ref, y1_ref, z1_ref, y0_ref, z0_ref,
    *rest,
):
    out_ref, m_hi, m_lo, s_hi, s_lo, sum_ref = rest[-6:]
    wide = SOURCES * BLOCK_FUNCTIONS

    @pl.when(pl.program_id(0) == 0)
    def _():
        split_store(m_hi, m_lo, slice(None), slice(0, wide), mix_ref[...])
        hamilton = (near_ref[...] + far_ref[...]) * weight_ref[...]
        split_store(m_hi, m_lo, slice(None), slice(wide, 2 * wide), hamilton)

    for rows in row_groups():
        for source in range(SOURCES):
            index, tile_of = turn_tables(place_ref, source, rows)
            for member in (1, 0):
                base = ((1 - member) * SOURCES + source) * BLOCK_FUNCTIONS
                near = slice(base + rows.start, base + rows.stop)
                for plane in range(step_planes):
                    cut = slice(plane * PATCH, plane * PATCH + LANES)
                    cut2 = slice(plane * PATCH + LANES, (plane + 1) * PATCH)
                    if source == 0:
                        first, second = own_ref[member, rows, cut], own_ref[member, rows, cut2]
                    else:
                        ref = ((y0_ref, z0_ref), (y1_ref, z1_ref))[member][source - 1]
                        first, second = ref[rows, cut], ref[rows, cut2]
                    tiles = placed_tiles(first, second, index, tile_of, source == 0)
                    for k in range(COLUMN_TILES):
                        at = (plane * COLUMN_TILES + k) * LANES
                        split_store(s_hi, s_lo, near, slice(at, at + LANES), tiles[k])
    dot = functools.partial(jnp.dot, preferred_element_type=jnp.float32)
    sum_ref[...] = dot(m_hi[...], s_hi[...]) + (dot(m_hi[...], s_lo[...]) + dot(m_lo[...], s_hi[...]))
    for rows in row_groups():
        lane = lax.broadcasted_iota(jnp.int32, (ROWS, LANES), 1)
        beyond = lane + jnp.broadcast_to(place_ref[rows, 0:1], (ROWS, LANES))
        index, inside = beyond & (LANES - 1), beyond < LANES
        for plane in range(step_planes):
            at = plane * COLUMN_TILES * LANES
            a, b, c = (
                lane_turn(sum_ref[rows, at + k * LANES : at + (k + 1) * LANES], index)
                for k in range(COLUMN_TILES)
            )
            out_ref[rows, plane * PATCH : plane * PATCH + LANES] = jnp.where(inside, a, b)
            out_ref[rows, plane * PATCH + LANES : (plane + 1) * PATCH] = jnp.where(inside, b, c)


def whole(shape):
    return pl.BlockSpec(shape, lambda i: (0,) * len(shape))


def gram(place, orbitals, y_part, z_part, before, start, planes, step):
    wide = SOURCES * BLOCK_FUNCTIONS
    width = step * PATCH
    lanes = step * COLUMN_TILES * LANES
    first = start // step
    return pl.pallas_call(
        functools.partial(gram_kernel, step),
        grid=(planes // step,),
        in_specs=[
            whole(place.shape),
            pl.BlockSpec((2, BLOCK_FUNCTIONS, width), lambda i: (0, 0, first + i)),
            pl.BlockSpec((BLOCK_FUNCTIONS, width), lambda i: (0, i)),
            pl.BlockSpec((BLOCK_FUNCTIONS, width), lambda i: (0, i)),
            whole((BLOCK_FUNCTIONS, wide)),
        ],
        out_specs=whole((BLOCK_FUNCTIONS, wide)),
        out_shape=jax.ShapeDtypeStruct((BLOCK_FUNCTIONS, wide), jnp.float32),
        scratch_shapes=[pltpu.VMEM((BLOCK_FUNCTIONS, lanes), jnp.bfloat16)] * 2
        + [pltpu.VMEM((wide, lanes), jnp.bfloat16)] * 2,
        cost_estimate=pl.CostEstimate(
            flops=6 * planes * BLOCK_FUNCTIONS * wide * COLUMN_TILES * LANES,
            bytes_accessed=4 * 4 * planes * PATCH * BLOCK_FUNCTIONS,
            transcendentals=0,
        ),
        compiler_params=pltpu.CompilerParams(vmem_limit_bytes=24 << 20),
        name="gram",
    )(place, orbitals, y_part, z_part, before)


def apply_part(place, mix, near, far, weight, orbitals, y1, z1, y0, z0, skip, held, start, planes, step):
    wide = SOURCES * BLOCK_FUNCTIONS
    width = step * PATCH
    lanes = step * COLUMN_TILES * LANES
    first = start // step
    behind = (start - skip) // step
    operands = [place, mix, near, far, weight, orbitals, y1, z1, y0, z0]
    small = whole((BLOCK_FUNCTIONS, wide))
    part = pl.BlockSpec((BLOCK_FUNCTIONS, width), lambda i: (0, behind + i))
    fresh = pl.BlockSpec((BLOCK_FUNCTIONS, width), lambda i: (0, i))
    in_specs = [
        whole(place.shape), small, small, small, whole(weight.shape),
        pl.BlockSpec((2, BLOCK_FUNCTIONS, width), lambda i: (0, 0, first + i)),
        part, part, fresh, fresh,
    ]
    aliases = {}
    if held is not None:
        aliases = {len(operands): 0}
        operands.append(held)
        in_specs.append(pl.BlockSpec(memory_space=pl.ANY))
    return pl.pallas_call(
        functools.partial(apply_kernel, step),
        grid=(planes // step,),
        in_specs=in_specs,
        out_specs=pl.BlockSpec((BLOCK_FUNCTIONS, width), lambda i: (0, first + i)),
        out_shape=jax.ShapeDtypeStruct(orbitals.shape[1:], jnp.float32),
        input_output_aliases=aliases,
        scratch_shapes=[pltpu.VMEM((BLOCK_FUNCTIONS, 2 * wide), jnp.bfloat16)] * 2
        + [pltpu.VMEM((2 * wide, lanes), jnp.bfloat16)] * 2
        + [pltpu.VMEM((BLOCK_FUNCTIONS, lanes), jnp.float32)],
        cost_estimate=pl.CostEstimate(
            flops=12 * planes * BLOCK_FUNCTIONS * wide * COLUMN_TILES * LANES,
            bytes_accessed=4 * 7 * planes * PATCH * BLOCK_FUNCTIONS,
            transcendentals=0,
        ),
        compiler_params=pltpu.CompilerParams(vmem_limit_bytes=24 << 20),
        name="apply",
    )(*operands)


FIRST_SHARES = (8, 8)
SECOND_SHARES = (8, 4, 4)


def per_device(orbitals, offsets, pairs, kernel):
    members, per_dev, seg_local = orbitals.shape
    planes = seg_local // PATCH
    groups = lax.axis_size("orb")
    slabs = lax.axis_size("slab")
    group = lax.axis_index("orb")
    odd = group % 2
    volume = 1.0 / math.sqrt(SEG)

    swap = [(at, at ^ 1) for at in range(groups)]
    onward = [(at, at + 2) for at in range(0, groups - 2, 2)]
    onward += [(at, at - 2) for at in range(3, groups, 2)]

    def sent(member, bounds):
        across, along = [], []
        for number, (start, stop) in enumerate(bounds):
            piece = orbitals[member, :, start * PATCH : stop * PATCH]
            with jax.named_scope(f"y{member}_{number}"):
                across.append(lax.ppermute(piece, "orb", swap))
            with jax.named_scope(f"z{member}_{number}"):
                along.append(lax.ppermute(across[-1], "orb", onward))
        return across, along

    first_bounds = chunk_bounds(planes, FIRST_SHARES)
    second_bounds = chunk_bounds(planes, SECOND_SHARES)
    y1, z1 = sent(1, first_bounds)
    y0, z0 = sent(0, second_bounds)

    signs = jnp.stack([jnp.int32(0), 1 - 2 * odd, 2 * odd - 1]).astype(jnp.int32)
    blocks = jnp.clip(group + signs, 0, groups - 1)
    shift = jnp.clip(
        offsets.reshape(groups, per_dev)[blocks] - BSTEP * blocks[:, None], 0, SPREAD
    )
    place = (shift + BSTEP * signs[:, None]).astype(jnp.int32).T

    slots = REACH + signs
    listed = pairs[0].astype(jnp.float32)[slots]
    mix = (kernel[0][slots] * listed[:, None, None]).transpose(1, 0, 2).reshape(per_dev, -1)
    weight = jnp.repeat(-volume * listed, per_dev)[None, :]

    total = jnp.zeros((per_dev, SOURCES * per_dev), jnp.float32)
    for number, (start, stop) in enumerate(first_bounds):
        total = gram(place, orbitals, y1[number], z1[number], total, start, stop - start, 2)
    far = None
    step = 1
    while step < slabs:
        if far is not None:
            total = total + far
        far = lax.ppermute(total, "slab", [(at, at ^ step) for at in range(slabs)])
        step *= 2

    held = None
    for number, (start, stop) in enumerate(second_bounds):
        inside = [at for at, (low, high) in enumerate(first_bounds) if low <= start and stop <= high][0]
        held = apply_part(
            place, mix, total, far, weight, orbitals, y1[inside], z1[inside], y0[number], z0[number],
            first_bounds[inside][0], held, start, stop - start, 2,
        )
    return held


def solution(mesh):
    placed = (P(None, "orb", "slab"), P(), P("orb", None), P("orb", None, None, None))
    return jax.shard_map(
        per_device, mesh=mesh, in_specs=placed, out_specs=P("orb", "slab"), check_vma=False
    )
```

```python
import functools
import math

import jax
import jax.numpy as jnp
from jax import lax
from jax.experimental import pallas as pl
from jax.experimental.pallas import tpu as pltpu
from jax.sharding import PartitionSpec as P


BLOCK_FUNCTIONS = 128
PATCH = 256
SPREAD = 128
REACH = 1
BSTEP = 192
SEG = 16384
LANES = 128
HALF = LANES // 2
ROWS = 32
TILES = (PATCH + SPREAD) // LANES
SLOTS = 2 * REACH + 1
WIDE = SLOTS * BLOCK_FUNCTIONS
PAIR = 2
OUTSIDE = 1 << 16
NT = (((1,), (1,)), ((), ()))


def bounds_of(planes, edges):
    marks = sorted({edge * planes // 16 // PAIR * PAIR for edge in edges})
    return list(zip(marks[:-1], marks[1:]))


def turned(values, index):
    return jnp.take_along_axis(values, index, axis=1)


def lane_of(rows=ROWS):
    return lax.broadcasted_iota(jnp.int32, (rows, LANES), 1)


def row_groups():
    return [slice(start, start + ROWS) for start in range(0, BLOCK_FUNCTIONS, ROWS)]


def halves(values):
    high = values.astype(jnp.bfloat16)
    return high, (values - high.astype(jnp.float32)).astype(jnp.bfloat16)


def pack_kernel(me_ref, box_ref, a_ref, b_ref):
    odd = me_ref[0] % 2
    for rows in row_groups():
        low = lane_of() < HALF
        split = []
        for plane in range(PAIR):
            whole_at = pl.multiple_of(plane * PATCH + odd * LANES, LANES)
            split_at = pl.multiple_of(plane * PATCH + (1 - odd) * LANES, LANES)
            a_ref[rows, plane * LANES : (plane + 1) * LANES] = box_ref[0, rows, pl.ds(whole_at, LANES)]
            split.append(box_ref[0, rows, pl.ds(split_at, LANES)])
        left = jnp.where(low, split[0], pltpu.roll(split[1], HALF, 1))
        right = jnp.where(low, pltpu.roll(split[0], HALF, 1), split[1])
        a_ref[rows, PAIR * LANES : TILES * LANES] = jnp.where(odd == 1, right, left)
        b_ref[rows, :] = jnp.where(odd == 1, left, right)


def packed(me, orbitals, member, start, stop):
    pairs_in = (stop - start) // PAIR
    first = start // PAIR
    return pl.pallas_call(
        pack_kernel,
        grid=(pairs_in,),
        in_specs=[
            pl.BlockSpec(memory_space=pltpu.SMEM),
            pl.BlockSpec((1, BLOCK_FUNCTIONS, PAIR * PATCH), lambda i: (member, 0, first + i)),
        ],
        out_specs=[
            pl.BlockSpec((BLOCK_FUNCTIONS, TILES * LANES), lambda i: (0, i)),
            pl.BlockSpec((BLOCK_FUNCTIONS, LANES), lambda i: (0, i)),
        ],
        out_shape=[
            jax.ShapeDtypeStruct((BLOCK_FUNCTIONS, pairs_in * TILES * LANES), jnp.float32),
            jax.ShapeDtypeStruct((BLOCK_FUNCTIONS, pairs_in * LANES), jnp.float32),
        ],
        cost_estimate=pl.CostEstimate(
            flops=0, bytes_accessed=8 * BLOCK_FUNCTIONS * pairs_in * PAIR * PATCH, transcendentals=0
        ),
        compiler_params=pltpu.CompilerParams(vmem_limit_bytes=60 << 20),
        name="pack",
    )(me, orbitals)


def make_tables(groups, me, offsets_ref, table_ref):
    upward = 1 - 2 * (me % 2)
    for source, sign in enumerate((0, upward, -upward)):
        block = me + sign
        row = jnp.clip(block, 0, groups - 1)
        shift = jnp.clip(offsets_ref[pl.ds(row, 1), :] - BSTEP * row, 0, SPREAD)
        if source > 0:
            shift = shift + jnp.where(sign > 0, BSTEP - LANES, -BSTEP)
            shift = shift + jnp.where(block == row, 0, OUTSIDE)
        table_ref[source] = jnp.broadcast_to(shift, (BLOCK_FUNCTIONS, LANES)).T


def own_tiles(table_ref, rows, first, second):
    ahead = lane_of() - table_ref[0, rows, :]
    index, inside = ahead & (LANES - 1), ahead >= 0
    left, right = turned(first, index), turned(second, index)
    zero = jnp.zeros_like(left)
    return jnp.where(inside, left, zero), jnp.where(inside, right, left), jnp.where(inside, zero, right)


def near_tiles(table_ref, source, rows, fixed, a_ref, b_ref):
    ahead = lane_of() - table_ref[source, rows, :]
    index = ahead & (LANES - 1)
    tile_of = ahead >> 7
    fixed_in = tile_of - fixed
    split_in = tile_of - (1 - fixed)
    within = index & (HALF - 1)
    shared = a_ref[rows, PAIR * LANES : TILES * LANES]
    result = []
    for plane in range(PAIR):
        whole = turned(a_ref[rows, plane * LANES : (plane + 1) * LANES], index)
        split = turned(shared, within + plane * HALF)
        if b_ref is not None:
            split = jnp.where((index >> 6) == fixed, split, turned(b_ref[rows, :], within + plane * HALF))
        zero = jnp.zeros_like(whole)
        result.append(
            tuple(
                jnp.where(fixed_in == -at, whole, jnp.where(split_in == -at, split, zero))
                for at in range(2)
            )
        )
    return result


def place_all(table_ref, odd, member, own_ref, ya_ref, yb_ref, za_ref, hi_ref, lo_ref):
    y_slot, z_slot = 2 * (1 - odd), 2 * odd
    for rows in row_groups():
        for plane in range(PAIR):
            lanes = slice(plane * LANES, (plane + 1) * LANES)
            cut = plane * PATCH
            tiles = own_tiles(
                table_ref, rows, own_ref[member, rows, cut : cut + LANES],
                own_ref[member, rows, cut + LANES : cut + PATCH],
            )
            stack = slice(BLOCK_FUNCTIONS + rows.start, BLOCK_FUNCTIONS + rows.stop)
            for k in range(TILES):
                hi_ref[k, stack, lanes], lo_ref[k, stack, lanes] = halves(tiles[k])
        for source, slot, a_ref, b_ref in ((1, y_slot, ya_ref, yb_ref), (2, z_slot, za_ref, None)):
            base = pl.multiple_of(slot * BLOCK_FUNCTIONS + rows.start, ROWS)
            first = slot // 2
            for plane, tiles in enumerate(near_tiles(table_ref, source, rows, 1 - odd, a_ref, b_ref)):
                lanes = slice(plane * LANES, (plane + 1) * LANES)
                for at in range(2):
                    high, low = halves(tiles[at])
                    hi_ref[first + at, pl.ds(base, ROWS), lanes] = high
                    lo_ref[first + at, pl.ds(base, ROWS), lanes] = low


def slots_of(k):
    start, stop = (0 if k < 2 else 1), (2 if k < 1 else 3)
    return slice(start * BLOCK_FUNCTIONS, stop * BLOCK_FUNCTIONS)


def mixed(m_hi, m_lo, s_hi, s_lo, k):
    part = slots_of(k)
    dot = functools.partial(jnp.dot, preferred_element_type=jnp.float32)
    return dot(m_hi[:, part], s_hi[k, part, :]) + (
        dot(m_hi[:, part], s_lo[k, part, :]) + dot(m_lo[:, part], s_hi[k, part, :])
    )


def gram_kernel(
    groups, me_ref, pairs_ref, offsets_ref, kernel_ref, own_ref, ya_ref, yb_ref, za_ref, before_ref,
    out_ref, sum_ref, table_ref, m_hi, m_lo, l_hi, l_lo, r_hi, r_lo,
):
    me = me_ref[0]

    @pl.when(pl.program_id(0) == 0)
    def _():
        make_tables(groups, me, offsets_ref, table_ref)
        for slot in range(SLOTS):
            part = slice(slot * BLOCK_FUNCTIONS, (slot + 1) * BLOCK_FUNCTIONS)
            m_hi[:, part], m_lo[:, part] = halves(kernel_ref[0, slot] * pairs_ref[0, slot].astype(jnp.float32))
        out_ref[...] = before_ref[...]

    for rows in row_groups():
        for plane in range(PAIR):
            lanes = slice(plane * LANES, (plane + 1) * LANES)
            cut = plane * PATCH
            tiles = own_tiles(
                table_ref, rows, own_ref[0, rows, cut : cut + LANES],
                own_ref[0, rows, cut + LANES : cut + PATCH],
            )
            for k in range(TILES):
                l_hi[k, rows, lanes], l_lo[k, rows, lanes] = halves(tiles[k])
    place_all(table_ref, me % 2, 1, own_ref, ya_ref, yb_ref, za_ref, r_hi, r_lo)
    dot = functools.partial(lax.dot_general, dimension_numbers=NT, preferred_element_type=jnp.float32)
    for k in range(TILES):
        part = slots_of(k)
        out_ref[:, part] += dot(l_hi[k], r_hi[k, part, :]) + (
            dot(l_hi[k], r_lo[k, part, :]) + dot(l_lo[k], r_hi[k, part, :])
        )
        sum_ref[:, k * PAIR * LANES : (k + 1) * PAIR * LANES] = mixed(m_hi, m_lo, r_hi, r_lo, k)


def apply_kernel(
    groups, volume, me_ref, pairs_ref, offsets_ref, near_ref, far_ref, own_ref, ya_ref, yb_ref, za_ref, sum_ref,
    *rest,
):
    out_ref, table_ref, m_hi, m_lo, s_hi, s_lo, acc_ref = rest[-7:]
    me = me_ref[0]

    @pl.when(pl.program_id(0) == 0)
    def _():
        make_tables(groups, me, offsets_ref, table_ref)
        for slot in range(SLOTS):
            part = slice(slot * BLOCK_FUNCTIONS, (slot + 1) * BLOCK_FUNCTIONS)
            weight = -volume * pairs_ref[0, slot].astype(jnp.float32)
            m_hi[:, part], m_lo[:, part] = halves((near_ref[:, part] + far_ref[:, part]) * weight)

    place_all(table_ref, me % 2, 0, own_ref, ya_ref, yb_ref, za_ref, s_hi, s_lo)
    for k in range(TILES):
        lanes = slice(k * PAIR * LANES, (k + 1) * PAIR * LANES)
        acc_ref[k] = sum_ref[:, lanes] + mixed(m_hi, m_lo, s_hi, s_lo, k)
    for rows in row_groups():
        beyond = lane_of() + table_ref[0, rows, :]
        index, inside = beyond & (LANES - 1), beyond < LANES
        for plane in range(PAIR):
            lanes = slice(plane * LANES, (plane + 1) * LANES)
            a, b, c = (turned(acc_ref[k, rows, lanes], index) for k in range(TILES))
            out_ref[rows, plane * PATCH : plane * PATCH + LANES] = jnp.where(inside, a, b)
            out_ref[rows, plane * PATCH + LANES : (plane + 1) * PATCH] = jnp.where(inside, b, c)


def whole(shape):
    return pl.BlockSpec(shape, lambda i: (0,) * len(shape))


SMEM = pl.BlockSpec(memory_space=pltpu.SMEM)
TABLES = pltpu.VMEM((3, BLOCK_FUNCTIONS, LANES), jnp.int32)


def stacks(depth):
    return [pltpu.VMEM((TILES, depth, PAIR * LANES), jnp.bfloat16)] * 2


def gram(me, pairs, offsets, kernel, orbitals, ya, yb, za, before, start, stop):
    first, steps = start // PAIR, (stop - start) // PAIR
    lanes = TILES * PAIR * LANES
    return pl.pallas_call(
        functools.partial(gram_kernel, offsets.shape[0]),
        grid=(steps,),
        in_specs=[
            SMEM, SMEM, whole(offsets.shape), whole(kernel.shape),
            pl.BlockSpec((2, BLOCK_FUNCTIONS, PAIR * PATCH), lambda i: (0, 0, first + i)),
            pl.BlockSpec((BLOCK_FUNCTIONS, TILES * LANES), lambda i: (0, i)),
            pl.BlockSpec((BLOCK_FUNCTIONS, LANES), lambda i: (0, i)),
            pl.BlockSpec((BLOCK_FUNCTIONS, TILES * LANES), lambda i: (0, i)),
            whole(before.shape),
        ],
        out_specs=[whole(before.shape), pl.BlockSpec((BLOCK_FUNCTIONS, lanes), lambda i: (0, i))],
        out_shape=[
            jax.ShapeDtypeStruct(before.shape, jnp.float32),
            jax.ShapeDtypeStruct((BLOCK_FUNCTIONS, steps * lanes), jnp.float32),
        ],
        scratch_shapes=[TABLES]
        + [pltpu.VMEM((BLOCK_FUNCTIONS, WIDE), jnp.bfloat16)] * 2
        + stacks(BLOCK_FUNCTIONS) + stacks(WIDE),
        cost_estimate=pl.CostEstimate(
            flops=12 * steps * BLOCK_FUNCTIONS * WIDE * lanes,
            bytes_accessed=4 * BLOCK_FUNCTIONS * steps * (4 * PAIR * PATCH + lanes),
            transcendentals=0,
        ),
        compiler_params=pltpu.CompilerParams(vmem_limit_bytes=16 << 20),
        name="gram",
    )(me, pairs, offsets, kernel, orbitals, ya, yb, za, before)


def applied(me, pairs, offsets, near, far, orbitals, ya, yb, za, sums, skip, held, start, stop):
    first, steps = start // PAIR, (stop - start) // PAIR
    behind = (start - skip) // PAIR
    lanes = TILES * PAIR * LANES
    operands = [me, pairs, offsets, near, far, orbitals, ya, yb, za, sums]
    in_specs = [
        SMEM, SMEM, whole(offsets.shape), whole(near.shape), whole(far.shape),
        pl.BlockSpec((1, BLOCK_FUNCTIONS, PAIR * PATCH), lambda i: (0, 0, first + i)),
        pl.BlockSpec((BLOCK_FUNCTIONS, TILES * LANES), lambda i: (0, i)),
        pl.BlockSpec((BLOCK_FUNCTIONS, LANES), lambda i: (0, i)),
        pl.BlockSpec((BLOCK_FUNCTIONS, TILES * LANES), lambda i: (0, i)),
        pl.BlockSpec((BLOCK_FUNCTIONS, lanes), lambda i: (0, behind + i)),
    ]
    aliases = {}
    if held is not None:
        aliases = {len(operands): 0}
        operands.append(held)
        in_specs.append(pl.BlockSpec(memory_space=pl.ANY))
    return pl.pallas_call(
        functools.partial(apply_kernel, offsets.shape[0], 1.0 / math.sqrt(SEG)),
        grid=(steps,),
        in_specs=in_specs,
        out_specs=pl.BlockSpec((BLOCK_FUNCTIONS, PAIR * PATCH), lambda i: (0, first + i)),
        out_shape=jax.ShapeDtypeStruct(orbitals.shape[1:], jnp.float32),
        input_output_aliases=aliases,
        scratch_shapes=[TABLES]
        + [pltpu.VMEM((BLOCK_FUNCTIONS, WIDE), jnp.bfloat16)] * 2
        + stacks(WIDE)
        + [pltpu.VMEM((TILES, BLOCK_FUNCTIONS, PAIR * LANES), jnp.float32)],
        cost_estimate=pl.CostEstimate(
            flops=6 * steps * BLOCK_FUNCTIONS * WIDE * lanes,
            bytes_accessed=4 * BLOCK_FUNCTIONS * steps * (4 * PAIR * PATCH + lanes),
            transcendentals=0,
        ),
        compiler_params=pltpu.CompilerParams(vmem_limit_bytes=16 << 20),
        name="apply",
    )(*operands)


FIRST_EDGES = (0, 6, 10, 16)
SECOND_EDGES = (0, 6, 10, 14, 16)


def per_device(orbitals, offsets, pairs, kernel):
    per_dev, planes = orbitals.shape[1], orbitals.shape[2] // PATCH
    groups, slabs = lax.axis_size("orb"), lax.axis_size("slab")
    assert per_dev == BLOCK_FUNCTIONS and groups % 2 == 0
    assert planes % PAIR == 0 and slabs & (slabs - 1) == 0
    me = lax.axis_index("orb").astype(jnp.int32)[None]
    offsets = offsets.reshape(groups, per_dev)

    swap = [(at, at ^ 1) for at in range(groups)]
    onward = [(at, (at + 2 - 4 * (at % 2)) % groups) for at in range(groups)]
    bounds = {1: bounds_of(planes, FIRST_EDGES), 0: bounds_of(planes, SECOND_EDGES)}

    ya, yb, za = {}, {}, {}
    for member in (1, 0):
        for number, (start, stop) in enumerate(bounds[member]):
            a, b = packed(me, orbitals, member, start, stop)
            ya[member, number] = lax.ppermute(a, "orb", swap)
            yb[member, number] = lax.ppermute(b, "orb", swap)
            za[member, number] = lax.ppermute(ya[member, number], "orb", onward)

    total, sums = jnp.zeros((per_dev, WIDE), jnp.float32), []
    for number, (start, stop) in enumerate(bounds[1]):
        parts = (ya[1, number], yb[1, number], za[1, number])
        total, part = gram(me, pairs, offsets, kernel, orbitals, *parts, total, start, stop)
        sums.append(part)
    far, step = jnp.zeros_like(total), 1
    while step < slabs:
        if step > 1:
            total = total + far
        far = lax.ppermute(total, "slab", [(at, at ^ step) for at in range(slabs)])
        step *= 2

    held = None
    for number, (start, stop) in enumerate(bounds[0]):
        [inside] = [at for at, (low, high) in enumerate(bounds[1]) if low <= start and stop <= high]
        parts = (ya[0, number], yb[0, number], za[0, number])
        held = applied(
            me, pairs, offsets, total, far, orbitals, *parts, sums[inside], bounds[1][inside][0],
            held, start, stop,
        )
    return held


def solution(mesh):
    placed = (P(None, "orb", "slab"), P(), P("orb", None), P("orb", None, None, None))
    return jax.shard_map(per_device, mesh=mesh, in_specs=placed, out_specs=P("orb", "slab"), check_vma=False)
```
